256 devices in a mesh: seq: 32 (over x, z), ch: 8 (over y, core).
Axes of the slice: x: 4, y: 4, z: 8, core: 2. Of those that a mesh axis runs over, the one named last changes fastest.
Arguments:
- query_rows: float32 [16384, 2048], P('seq', 'ch'), may hold values from -6 to 6
- key_rows: float32 [16384, 2048], P('seq', 'ch'), may hold values from -6 to 6
- value_rows: float32 [16384, 2048], P('seq', 'ch'), may hold values from -6 to 6
- filters: float32 [16384, 2048], P('seq', 'ch'), may hold values from -0.046875 to 0.046875
- skip_gain: float32 [2048], P('ch'), may hold values from -4 to 4
- out_weight: float32 [2048, 2048], P('ch'), may hold values from -0.125 to 0.125
Outputs:
- projected: float32 [2048, 16384], P('ch', 'seq')
The draws below stay inside these ranges and needn't reach their ends.
All inputs are finite; a program needn't handle non-finite values.
Results may differ from the reference program's by a relative error of at most 0.00007.
Values sent between devices are 32-bit elements; how exact they have to be, the bound alone decides.
A program may use at most 64 MiB of HBM per device.

```python
import jax
import jax.numpy as jnp
from jax import lax

C = 2048
SEQ = 16384


def shard_levels(rng, shape, shards, least, top_value):
    def one(dim, parts):
        draws = jax.random.uniform(jax.random.fold_in(jax.random.fold_in(rng, 6), dim), (parts,), jnp.float32, least / len(shards), top_value / len(shards))
        return jnp.repeat(jnp.exp(draws), shape[dim] // parts).reshape((-1,) + (1,) * (len(shape) - dim - 1))

    gain = one(*shards[0])
    for cut in shards[1:]:
        gain = gain * one(*cut)
    return gain


def centred(own_key, dims, scale, reach, split=(), kind=jnp.bfloat16):
    array = scale * jax.random.normal(own_key, dims, jnp.float32)
    if split:
        array = array * shard_levels(own_key, dims, split, -0.22, 0.18)
    return jnp.clip(array, -reach, reach).astype(kind)


def setup_inputs(seed: int = 0) -> dict:
    seeds = jax.random.split(jax.random.key(seed), 7)
    query_rows = centred(seeds[0], (SEQ, C), 1.0, 6.0, ((0, 32), (1, 8)), jnp.float32)
    key_rows = centred(seeds[1], (SEQ, C), 1.0, 6.0, ((0, 32), (1, 8)), jnp.float32)
    value_rows = centred(seeds[2], (SEQ, C), 1.0, 6.0, ((0, 32), (1, 8)), jnp.float32)
    filters = centred(seeds[3], (SEQ, C), SEQ ** -0.5, 0.046875, ((0, 32), (1, 8)), jnp.float32)
    skip_gain = centred(seeds[4], (C,), 1.0, 4.0, ((0, 8),), jnp.float32)
    out_weight = centred(seeds[5], (C, C), C ** -0.5, 0.125, ((0, 8),), jnp.float32)
    return dict(query_rows=query_rows, key_rows=key_rows, value_rows=value_rows, filters=filters, skip_gain=skip_gain, out_weight=out_weight)


def reference(query_rows, key_rows, value_rows, filters, skip_gain, out_weight):
    gated = key_rows * value_rows
    period = 2 * SEQ
    spectrum = jnp.fft.rfft(gated, n=period, axis=0) * jnp.fft.rfft(filters, n=period, axis=0)
    convolved = jnp.fft.irfft(spectrum, n=period, axis=0)[:SEQ].astype(gated.dtype)
    mixed = query_rows * (convolved + skip_gain[None, :] * gated)
    return jnp.dot(out_weight.T, mixed.T, precision=lax.Precision.HIGHEST, preferred_element_type=jnp.float32)
```

```python
import functools
import math

import jax
import jax.numpy as jnp
import numpy as np
from jax import lax
from jax.experimental import pallas as pl
from jax.experimental.pallas import tpu as pltpu
from jax.sharding import PartitionSpec as P

CHUNKS = 2
LANES = 128
MESH = pl.DeviceIdType.MESH


def split_table(table):
    high = table.astype(jnp.bfloat16)
    low = (table - high.astype(np.float64)).astype(jnp.bfloat16)
    return high, low


def tables(parts, per_part):
    rows = parts * per_part
    period = 2 * rows * LANES
    odd = np.arange(rows) + 0.5
    outer = 2 * math.pi * odd[:, None] * np.arange(rows)[None, :] / (2 * rows)
    first = np.zeros((2, 2, rows, parts, 2, per_part))
    for pair in range(2):
        first[0, pair, :, :, pair, :] = np.cos(outer).reshape(rows, parts, per_part)
        first[1, pair, :, :, pair, :] = -np.sin(outer).reshape(rows, parts, per_part)
    first = first.reshape(4 * rows, 2 * rows)
    last = first.T * (2.0 / period)
    turn = 2 * math.pi * odd[:, None] * np.arange(LANES)[None, :] / period
    turn_cos = np.tile(np.cos(turn), (2, 2)).astype(np.float32)
    turn_sin = np.tile(np.sin(turn), (2, 2)).astype(np.float32)
    inner = 2 * math.pi * (np.arange(LANES)[:, None] * np.arange(LANES)[None, :] % LANES) / LANES
    cos, sin = np.cos(inner), np.sin(inner)
    ahead = np.block([[cos, -sin], [sin, cos]])
    behind = np.block([[cos, sin], [-sin, cos]])
    return (
        *split_table(first),
        *split_table(last),
        *split_table(ahead),
        *split_table(behind),
        turn_cos,
        turn_sin,
    )


def split(value):
    high = value.astype(jnp.bfloat16)
    low = (value - high.astype(jnp.float32)).astype(jnp.bfloat16)
    return high, low


def dot(a, b):
    return jnp.dot(a, b, preferred_element_type=jnp.float32)


def dot3(a, b):
    return dot(a[0], b[0]) + dot(a[0], b[1]) + dot(a[1], b[0])


def convolve_pair(data, first, last, ahead, behind, turn_cos, turn_sin):
    half = data.shape[0]
    stage = dot3(first, split(data))
    re, im = stage[:half], stage[half:]
    cos, sin = turn_cos[...], turn_sin[...]
    re, im = re * cos + im * sin, im * cos - re * sin
    stage = jnp.concatenate(
        [
            jnp.concatenate([re[:, :LANES], im[:, :LANES]], axis=1),
            jnp.concatenate([re[:, LANES:], im[:, LANES:]], axis=1),
        ],
        axis=0,
    )
    stage = dot3(split(stage), ahead)
    gre, gim = stage[:half, :LANES], stage[:half, LANES:]
    fre, fim = stage[half:, :LANES], stage[half:, LANES:]
    stage = jnp.concatenate([gre * fre - gim * fim, gre * fim + gim * fre], axis=1)
    stage = dot3(split(stage), behind)
    re, im = stage[:, :LANES], stage[:, LANES:]
    cos, sin = cos[:, :LANES], sin[:, :LANES]
    stage = jnp.concatenate([re * cos - im * sin, im * cos + re * sin], axis=0)
    return dot3(last, split(stage))


def kernel(
    parts,
    ys,
    query_hbm,
    key_hbm,
    value_hbm,
    filter_hbm,
    skip_hbm,
    weight_hbm,
    *rest,
):
    table_hbm, rest = rest[:10], rest[10:]
    out_ref, rest = rest[0], rest[1:]
    table_ref, rest = rest[:10], rest[10:]
    (
        query_in,
        key_in,
        value_in,
        filter_in,
        skip_in,
        query_t,
        sent,
        got,
        conv_sent,
        conv_got,
        weights,
        weight_t,
        mixed,
        total,
        partner_got,
        load_sem,
        table_sem,
        send_sem,
        recv_sem,
        conv_send_sem,
        conv_recv_sem,
        weight_send_sem,
        weight_recv_sem,
        mixed_send_sem,
        mixed_recv_sem,
        partner_send_sem,
        partner_recv_sem,
    ) = rest
    length, channels = query_in.shape
    per_part = length // LANES
    chunk_channels = channels // CHUNKS
    slab = chunk_channels // parts * per_part
    outs = weights.shape[2]
    me = lax.axis_index("seq")
    lane = lax.axis_index("ch")
    core = lax.rem(lane, 2)
    own_y = lane // 2
    partner = lane + 1 - 2 * core
    own_half = pl.multiple_of(core * (outs // 2), outs // 2)
    partner_half = pl.multiple_of((1 - core) * (outs // 2), outs // 2)

    loads = [
        pltpu.make_async_copy(source, target, load_sem.at[number])
        for number, (source, target) in enumerate(
            [
                (filter_hbm, filter_in),
                (skip_hbm, skip_in),
                (key_hbm, key_in),
                (value_hbm, value_in),
                (query_hbm, query_in),
            ]
        )
    ]
    for load in loads[:4]:
        load.start()

    barrier = pltpu.get_barrier_semaphore()

    @pl.loop(1, parts)
    def _(step):
        pl.semaphore_signal(
            barrier, inc=1, device_id={"seq": lax.rem(me + step, parts)}, device_id_type=MESH
        )

    @pl.loop(1, ys)
    def _(step):
        pl.semaphore_signal(
            barrier, inc=1, device_id={"ch": lax.rem(lane + 2 * step, 2 * ys)}, device_id_type=MESH
        )

    pl.semaphore_signal(barrier, inc=1, device_id={"ch": partner}, device_id_type=MESH)

    loads[4].start()
    table_loads = [
        pltpu.make_async_copy(source, target, table_sem.at[number])
        for number, (source, target) in enumerate(zip(table_hbm, table_ref))
    ]
    for load in table_loads:
        load.start()

    def place(source, which, columns):
        for row in range(per_part):
            block = source(pl.ds(row * LANES, LANES), pl.ds(columns, LANES))
            sent[which, pl.ds(columns * per_part + row, LANES, stride=per_part), :] = block.T

    for load in loads[:4]:
        load.wait()
    tap = jnp.where(me == 0, 1.0, 0.0).astype(jnp.float32)
    filter_in[0:1, :] = filter_in[0:1, :] + tap * skip_in[...]

    def send_chunk(chunk):
        for which in range(2):

            @pl.loop(1, parts)
            def _(step):
                peer = lax.rem(me + step, parts)
                start = pl.multiple_of(chunk * parts * slab + peer * slab, slab)
                pltpu.make_async_remote_copy(
                    src_ref=sent.at[which, pl.ds(start, slab), :],
                    dst_ref=got.at[which, chunk, me],
                    send_sem=send_sem.at[which, chunk],
                    recv_sem=recv_sem.at[which, chunk],
                    device_id={"seq": peer},
                    device_id_type=MESH,
                ).start()

            start = pl.multiple_of(chunk * parts * slab + me * slab, slab)
            pltpu.make_async_copy(
                sent.at[which, pl.ds(start, slab), :],
                got.at[which, chunk, me],
                recv_sem.at[which, chunk],
            ).start()

    def gated(rows, columns):
        return key_in[rows, columns] * value_in[rows, columns]

    def plain(rows, columns):
        return filter_in[rows, columns]

    sent_chunks = 0
    for columns in range(0, channels, LANES):
        place(plain, 1, columns)
        place(gated, 0, columns)
        if columns == 0:
            pl.semaphore_wait(barrier, parts - 1 + ys - 1 + 1)
        while (sent_chunks + 1) * chunk_channels <= columns + LANES:
            send_chunk(sent_chunks)
            sent_chunks += 1

    def weight_copy(step):
        peer_y = lax.rem(own_y + step, ys)
        start = pl.multiple_of(peer_y * outs, outs)
        return pltpu.make_async_remote_copy(
            src_ref=weight_hbm.at[:, pl.ds(start, outs)],
            dst_ref=weights.at[own_y],
            send_sem=weight_send_sem.at[step - 1],
            recv_sem=weight_recv_sem.at[step - 1],
            device_id={"ch": lax.rem(lane + 2 * step, 2 * ys)},
            device_id_type=MESH,
        )

    for step in range(1, ys):
        weight_copy(step).start()
    own_weight = pltpu.make_async_copy(
        weight_hbm.at[:, pl.ds(pl.multiple_of(own_y * outs, outs), outs)],
        weights.at[own_y],
        weight_recv_sem.at[ys - 1],
    )
    own_weight.start()

    loads[4].wait()
    for columns in range(0, channels, LANES):
        for row in range(per_part):
            query_t[pl.ds(columns, LANES), pl.ds(row * LANES, LANES)] = query_in[
                pl.ds(row * LANES, LANES), pl.ds(columns, LANES)
            ].T
    for load in table_loads:
        load.wait()

    first, last, ahead, behind = (
        (table_ref[2 * n][...], table_ref[2 * n + 1][...]) for n in range(4)
    )
    turn_cos, turn_sin = table_ref[8], table_ref[9]

    @pl.loop(0, CHUNKS)
    def _(chunk):
        for which in range(2):
            pltpu.make_async_copy(
                got.at[which, chunk], got.at[which, chunk], recv_sem.at[which, chunk]
            ).wait()

        @pl.loop(0, slab // 8)
        def _(pair):
            rows = pl.ds(pl.multiple_of(pair * 8, 8), 8)
            data = jnp.concatenate(
                [got[which, chunk, :, rows, :].reshape(parts * 8, LANES) for which in range(2)],
                axis=1,
            )
            done = convolve_pair(data, first, last, ahead, behind, turn_cos, turn_sin)
            conv_sent[chunk, :, rows, :] = done.reshape(parts, 8, LANES)

        place_at = pl.ds(pl.multiple_of(me * slab, slab), slab)

        @pl.loop(1, parts)
        def _(step):
            peer = lax.rem(me + step, parts)
            pltpu.make_async_remote_copy(
                src_ref=conv_sent.at[chunk, peer],
                dst_ref=conv_got.at[chunk, place_at, :],
                send_sem=conv_send_sem.at[chunk],
                recv_sem=conv_recv_sem.at[chunk],
                device_id={"seq": peer},
                device_id_type=MESH,
            ).start()

        pltpu.make_async_copy(
            conv_sent.at[chunk, me], conv_got.at[chunk, place_at, :], conv_recv_sem.at[chunk]
        ).start()

    own_weight.wait()
    for step in range(1, ys):
        weight_copy(step).wait_recv()

    @pl.loop(0, ys)
    def _(y):
        for chunk in range(CHUNKS):
            for out in range(0, outs, LANES):
                block = weights[y, pl.ds(chunk * chunk_channels, chunk_channels), pl.ds(out, LANES)].T
                high, low = split(block)
                weight_t[y, chunk, pl.ds(out, LANES), :] = jnp.concatenate([high, low, high], axis=1)

    total[...] = jnp.zeros_like(total)

    def mixed_copy(chunk, step):
        return pltpu.make_async_remote_copy(
            src_ref=mixed.at[own_y, chunk],
            dst_ref=mixed.at[own_y, chunk],
            send_sem=mixed_send_sem.at[chunk, step - 1],
            recv_sem=mixed_recv_sem.at[chunk, step - 1],
            device_id={"ch": lax.rem(lane + 2 * step, 2 * ys)},
            device_id_type=MESH,
        )

    def project(y, chunk):
        high, low = split(mixed[y, chunk])
        data = jnp.concatenate([high, high, low], axis=0)
        total[...] += dot(weight_t[y, chunk], data)

    @pl.loop(0, CHUNKS)
    def _(chunk):
        pltpu.make_async_copy(
            conv_got.at[chunk], conv_got.at[chunk], conv_recv_sem.at[chunk]
        ).wait()
        rows = pl.ds(pl.multiple_of(chunk * chunk_channels, chunk_channels), chunk_channels)
        for row in range(per_part):
            columns = pl.ds(row * LANES, LANES)
            mixed[own_y, chunk, :, columns] = (
                conv_got[chunk, pl.ds(row, chunk_channels, stride=per_part), :]
                * query_t[rows, columns]
            )
        for step in range(1, ys):
            mixed_copy(chunk, step).start()
        project(own_y, chunk)

    @pl.loop(0, CHUNKS)
    def _(chunk):
        for step in range(1, ys):
            mixed_copy(chunk, step).wait_recv()
            project(lax.rem(own_y + ys - step, ys), chunk)

    to_partner = pltpu.make_async_remote_copy(
        src_ref=total.at[pl.ds(partner_half, outs // 2), :],
        dst_ref=partner_got,
        send_sem=partner_send_sem,
        recv_sem=partner_recv_sem,
        device_id={"ch": partner},
        device_id_type=MESH,
    )
    to_partner.start()

    @pl.loop(0, CHUNKS)
    def _(chunk):
        for which in range(2):
            rest_of = got.at[which, chunk, pl.ds(0, parts - 1)]
            pltpu.make_async_copy(rest_of, rest_of, send_sem.at[which, chunk]).wait()
        rest_of = conv_sent.at[chunk, pl.ds(0, parts - 1)]
        pltpu.make_async_copy(rest_of, rest_of, conv_send_sem.at[chunk]).wait()
        for step in range(1, ys):
            mixed_copy(chunk, step).wait_send()

    for step in range(1, ys):
        weight_copy(step).wait_send()
    to_partner.wait()
    out_ref[...] = total[pl.ds(own_half, outs // 2), :] + partner_got[...]


def per_device(query_rows, key_rows, value_rows, filters, skip_gain, out_weight):
    parts = lax.axis_size("seq")
    ys = lax.axis_size("ch") // 2
    length, channels = query_rows.shape
    per_part = length // LANES
    outs = out_weight.shape[1] // ys
    chunk_channels = channels // CHUNKS
    slab = chunk_channels // parts * per_part
    consts = tables(parts, per_part)
    f32 = jnp.float32
    dma = pltpu.SemaphoreType.DMA
    return pl.pallas_call(
        functools.partial(kernel, parts, ys),
        out_shape=jax.ShapeDtypeStruct((outs // 2, length), f32),
        in_specs=[pl.BlockSpec(memory_space=pl.ANY)] * (6 + len(consts)),
        out_specs=pl.BlockSpec(memory_space=pltpu.VMEM),
        scratch_shapes=[
            *[pltpu.VMEM(table.shape, table.dtype) for table in consts],
            pltpu.VMEM((length, channels), f32),
            pltpu.VMEM((length, channels), f32),
            pltpu.VMEM((length, channels), f32),
            pltpu.VMEM((length, channels), f32),
            pltpu.VMEM((1, channels), f32),
            pltpu.VMEM((channels, length), f32),
            pltpu.VMEM((2, channels * per_part, LANES), f32),
            pltpu.VMEM((2, CHUNKS, parts, slab, LANES), f32),
            pltpu.VMEM((CHUNKS, parts, slab, LANES), f32),
            pltpu.VMEM((CHUNKS, parts * slab, LANES), f32),
            pltpu.VMEM((ys, channels, outs), f32),
            pltpu.VMEM((ys, CHUNKS, outs, 3 * chunk_channels), jnp.bfloat16),
            pltpu.VMEM((ys, CHUNKS, chunk_channels, length), f32),
            pltpu.VMEM((outs, length), f32),
            pltpu.VMEM((outs // 2, length), f32),
            dma((5,)),
            dma((len(consts),)),
            dma((2, CHUNKS)),
            dma((2, CHUNKS)),
            dma((CHUNKS,)),
            dma((CHUNKS,)),
            dma((ys - 1,)),
            dma((ys,)),
            dma((CHUNKS, ys - 1)),
            dma((CHUNKS, ys - 1)),
            dma(()),
            dma(()),
        ],
        compiler_params=pltpu.CompilerParams(collective_id=0, has_side_effects=True),
    )(
        query_rows,
        key_rows,
        value_rows,
        filters,
        skip_gain.reshape(1, channels),
        out_weight,
        *[jnp.asarray(table) for table in consts],
    )


def solution(mesh):
    in_specs = (
        P("seq", "ch"),
        P("seq", "ch"),
        P("seq", "ch"),
        P("seq", "ch"),
        P("ch"),
        P("ch", None),
    )
    out_specs = P("ch", "seq")
    return jax.shard_map(
        per_device, mesh=mesh, in_specs=in_specs, out_specs=out_specs, check_vma=False
    )
```

```python
import functools
import math

import jax
import jax.numpy as jnp
import numpy as np
from jax import lax
from jax.experimental import pallas as pl
from jax.experimental.pallas import tpu as pltpu
from jax.sharding import PartitionSpec as P

CHUNKS = 4
HELD = 1
LAG = CHUNKS - 1 - HELD
LANES = 128
MESH = pl.DeviceIdType.MESH


def split_table(table):
    high = table.astype(jnp.bfloat16)
    low = (table - high.astype(np.float64)).astype(jnp.bfloat16)
    return high, low


def tables(parts, per_part):
    rows = parts * per_part
    period = 2 * rows * LANES
    odd = np.arange(rows) + 0.5
    outer = 2 * math.pi * odd[:, None] * np.arange(rows)[None, :] / (2 * rows)
    first = np.zeros((2, 2, rows, parts, 2, per_part))
    for pair in range(2):
        first[0, pair, :, :, pair, :] = np.cos(outer).reshape(rows, parts, per_part)
        first[1, pair, :, :, pair, :] = -np.sin(outer).reshape(rows, parts, per_part)
    first = first.reshape(4 * rows, 2 * rows)
    last = first.T * (2.0 / period)
    turn = 2 * math.pi * odd[:, None] * np.arange(LANES)[None, :] / period
    turn_cos = np.tile(np.cos(turn), (2, 2)).astype(np.float32)
    turn_sin = np.tile(np.sin(turn), (2, 2)).astype(np.float32)
    inner = 2 * math.pi * (np.arange(LANES)[:, None] * np.arange(LANES)[None, :] % LANES) / LANES
    cos, sin = np.cos(inner), np.sin(inner)
    ahead = np.block([[cos, -sin], [sin, cos]])
    behind = np.block([[cos, sin], [-sin, cos]])
    return (
        *split_table(first),
        *split_table(last),
        *split_table(ahead),
        *split_table(behind),
        turn_cos,
        turn_sin,
    )


def split(value):
    high = value.astype(jnp.bfloat16)
    low = (value - high.astype(jnp.float32)).astype(jnp.bfloat16)
    return high, low


def dot(a, b):
    return jnp.dot(a, b, preferred_element_type=jnp.float32)


def dot3(a, b):
    return dot(a[0], b[0]) + dot(a[0], b[1]) + dot(a[1], b[0])


def convolve_pair(data, first, last, ahead, behind, turn_cos, turn_sin):
    half = data.shape[0]
    stage = dot3(first, split(data))
    re, im = stage[:half], stage[half:]
    cos, sin = turn_cos[...], turn_sin[...]
    re, im = re * cos + im * sin, im * cos - re * sin
    stage = jnp.concatenate(
        [
            jnp.concatenate([re[:, :LANES], im[:, :LANES]], axis=1),
            jnp.concatenate([re[:, LANES:], im[:, LANES:]], axis=1),
        ],
        axis=0,
    )
    stage = dot3(split(stage), ahead)
    gre, gim = stage[:half, :LANES], stage[:half, LANES:]
    fre, fim = stage[half:, :LANES], stage[half:, LANES:]
    stage = jnp.concatenate([gre * fre - gim * fim, gre * fim + gim * fre], axis=1)
    stage = dot3(split(stage), behind)
    re, im = stage[:, :LANES], stage[:, LANES:]
    cos, sin = cos[:, :LANES], sin[:, :LANES]
    stage = jnp.concatenate([re * cos - im * sin, im * cos + re * sin], axis=0)
    return dot3(last, split(stage))


def kernel(
    parts,
    ys,
    query_hbm,
    key_hbm,
    value_hbm,
    filter_hbm,
    skip_hbm,
    weight_hbm,
    *rest,
):
    table_hbm, rest = rest[:10], rest[10:]
    out_ref, rest = rest[0], rest[1:]
    table_ref, rest = rest[:10], rest[10:]
    (
        query_in,
        key_in,
        value_in,
        filter_in,
        skip_in,
        query_t,
        sent,
        got,
        conv_sent,
        conv_got,
        weights,
        weight_t,
        mixed,
        total,
        partner_got,
        load_sem,
        table_sem,
        send_sem,
        recv_sem,
        conv_send_sem,
        conv_recv_sem,
        weight_send_sem,
        weight_recv_sem,
        mixed_send_sem,
        mixed_recv_sem,
        partner_send_sem,
        partner_recv_sem,
    ) = rest
    length, channels = query_in.shape
    per_part = length // LANES
    chunk_channels = channels // CHUNKS
    slab = chunk_channels // parts * per_part
    outs = weights.shape[2]
    me = lax.axis_index("seq")
    lane = lax.axis_index("ch")
    core = lax.rem(lane, 2)
    own_y = lane // 2
    partner = lane + 1 - 2 * core
    own_half = pl.multiple_of(core * (outs // 2), outs // 2)
    partner_half = pl.multiple_of((1 - core) * (outs // 2), outs // 2)

    loads = [
        pltpu.make_async_copy(source, target, load_sem.at[number])
        for number, (source, target) in enumerate(
            [
                (filter_hbm, filter_in),
                (skip_hbm, skip_in),
                (key_hbm, key_in),
                (value_hbm, value_in),
                (query_hbm, query_in),
            ]
        )
    ]
    for load in loads[:4]:
        load.start()

    barrier = pltpu.get_barrier_semaphore()

    @pl.loop(1, parts)
    def _(step):
        pl.semaphore_signal(
            barrier, inc=1, device_id={"seq": lax.rem(me + step, parts)}, device_id_type=MESH
        )

    @pl.loop(1, ys)
    def _(step):
        pl.semaphore_signal(
            barrier, inc=1, device_id={"ch": lax.rem(lane + 2 * step, 2 * ys)}, device_id_type=MESH
        )

    pl.semaphore_signal(barrier, inc=1, device_id={"ch": partner}, device_id_type=MESH)

    loads[4].start()
    table_loads = [
        pltpu.make_async_copy(source, target, table_sem.at[number])
        for number, (source, target) in enumerate(zip(table_hbm, table_ref))
    ]
    for load in table_loads:
        load.start()

    def place(source, which, columns):
        for row in range(per_part):
            block = source(pl.ds(row * LANES, LANES), pl.ds(columns, LANES))
            sent[which, pl.ds(columns * per_part + row, LANES, stride=per_part), :] = block.T

    for load in loads[:4]:
        load.wait()
    tap = jnp.where(me == 0, 1.0, 0.0).astype(jnp.float32)
    filter_in[0:1, :] = filter_in[0:1, :] + tap * skip_in[...]

    def send_chunk(chunk):
        for which in range(2):

            @pl.loop(1, parts)
            def _(step):
                peer = lax.rem(me + step, parts)
                start = pl.multiple_of(chunk * parts * slab + peer * slab, slab)
                pltpu.make_async_remote_copy(
                    src_ref=sent.at[which, pl.ds(start, slab), :],
                    dst_ref=got.at[which, chunk, me],
                    send_sem=send_sem.at[which, chunk],
                    recv_sem=recv_sem.at[which, chunk],
                    device_id={"seq": peer},
                    device_id_type=MESH,
                ).start()

            start = pl.multiple_of(chunk * parts * slab + me * slab, slab)
            pltpu.make_async_copy(
                sent.at[which, pl.ds(start, slab), :],
                got.at[which, chunk, me],
                recv_sem.at[which, chunk],
            ).start()

    def gated(rows, columns):
        return key_in[rows, columns] * value_in[rows, columns]

    def plain(rows, columns):
        return filter_in[rows, columns]

    def weight_copy(step):
        peer_y = lax.rem(own_y + step, ys)
        start = pl.multiple_of(peer_y * outs, outs)
        return pltpu.make_async_remote_copy(
            src_ref=weight_hbm.at[:, pl.ds(start, outs)],
            dst_ref=weights.at[own_y],
            send_sem=weight_send_sem.at[step - 1],
            recv_sem=weight_recv_sem.at[step - 1],
            device_id={"ch": lax.rem(lane + 2 * step, 2 * ys)},
            device_id_type=MESH,
        )

    own_weight = pltpu.make_async_copy(
        weight_hbm.at[:, pl.ds(pl.multiple_of(own_y * outs, outs), outs)],
        weights.at[own_y],
        weight_recv_sem.at[ys - 1],
    )
    sent_chunks = 0
    for columns in range(0, channels, LANES):
        place(plain, 1, columns)
        place(gated, 0, columns)
        if columns == 0:
            pl.semaphore_wait(barrier, parts - 1 + ys - 1 + 1)
            for step in range(1, ys):
                weight_copy(step).start()
            own_weight.start()
        while (sent_chunks + 1) * chunk_channels <= columns + LANES:
            if sent_chunks < CHUNKS - HELD:
                send_chunk(sent_chunks)
            sent_chunks += 1

    loads[4].wait()
    for columns in range(0, channels, LANES):
        for row in range(per_part):
            query_t[pl.ds(columns, LANES), pl.ds(row * LANES, LANES)] = query_in[
                pl.ds(row * LANES, LANES), pl.ds(columns, LANES)
            ].T
    for load in table_loads:
        load.wait()

    first, last, ahead, behind = (
        (table_ref[2 * n][...], table_ref[2 * n + 1][...]) for n in range(4)
    )
    turn_cos, turn_sin = table_ref[8], table_ref[9]

    def prepare_weights():
        own_weight.wait()
        for step in range(1, ys):
            weight_copy(step).wait_recv()

        @pl.loop(0, ys)
        def _(y):
            for chunk in range(CHUNKS):
                for out in range(0, outs, LANES):
                    block = weights[y, pl.ds(chunk * chunk_channels, chunk_channels), pl.ds(out, LANES)].T
                    high, low = split(block)
                    weight_t[y, chunk, pl.ds(out, LANES), :] = jnp.concatenate([high, low, high], axis=1)

    def convolve_chunk(chunk):
        for which in range(2):
            pltpu.make_async_copy(
                got.at[which, chunk], got.at[which, chunk], recv_sem.at[which, chunk]
            ).wait()

        @pl.loop(0, slab // 8)
        def _(pair):
            rows = pl.ds(pl.multiple_of(pair * 8, 8), 8)
            data = jnp.concatenate(
                [got[which, chunk, :, rows, :].reshape(parts * 8, LANES) for which in range(2)],
                axis=1,
            )
            done = convolve_pair(data, first, last, ahead, behind, turn_cos, turn_sin)
            conv_sent[chunk, :, rows, :] = done.reshape(parts, 8, LANES)

        place_at = pl.ds(pl.multiple_of(me * slab, slab), slab)

        @pl.loop(1, parts)
        def _(step):
            peer = lax.rem(me + step, parts)
            pltpu.make_async_remote_copy(
                src_ref=conv_sent.at[chunk, peer],
                dst_ref=conv_got.at[chunk, place_at, :],
                send_sem=conv_send_sem.at[chunk],
                recv_sem=conv_recv_sem.at[chunk],
                device_id={"seq": peer},
                device_id_type=MESH,
            ).start()

        pltpu.make_async_copy(
            conv_sent.at[chunk, me], conv_got.at[chunk, place_at, :], conv_recv_sem.at[chunk]
        ).start()

        @pl.when(chunk < HELD)
        def _():
            send_chunk(chunk + CHUNKS - HELD)

    total[...] = jnp.zeros_like(total)

    ahead_y, behind_y = lax.rem(own_y + 1, ys), lax.rem(own_y + ys - 1, ys)
    across_y = lax.rem(own_y + 2, ys)
    half_rows = chunk_channels // 2

    def mixed_copy(chunk, owner, half, up, slot):
        return pltpu.make_async_remote_copy(
            src_ref=mixed.at[owner, chunk, pl.ds(half * half_rows, half_rows), :],
            dst_ref=mixed.at[owner, chunk, pl.ds(half * half_rows, half_rows), :],
            send_sem=mixed_send_sem.at[chunk, slot],
            recv_sem=mixed_recv_sem.at[chunk, slot],
            device_id={"ch": lax.rem(lane + (2 if up else 2 * ys - 2), 2 * ys)},
            device_id_type=MESH,
        )

    def own_copies(chunk):
        return [
            mixed_copy(chunk, own_y, 0, True, 0),
            mixed_copy(chunk, own_y, 1, False, 1),
            mixed_copy(chunk, own_y, 1, True, 2),
            mixed_copy(chunk, own_y, 0, False, 3),
        ]

    def relay_copies(chunk):
        return [
            mixed_copy(chunk, behind_y, 0, True, 4),
            mixed_copy(chunk, ahead_y, 1, False, 5),
        ]

    def project(y, chunk):
        high, low = split(mixed[y, chunk])
        data = jnp.concatenate([high, high, low], axis=0)
        total[...] += dot(weight_t[y, chunk], data)

    def relay(chunk):
        mixed_copy(chunk, own_y, 0, True, 0).wait_recv()
        mixed_copy(chunk, behind_y, 0, True, 4).start()
        mixed_copy(chunk, own_y, 1, False, 1).wait_recv()
        mixed_copy(chunk, ahead_y, 1, False, 5).start()

    def finish(chunk):
        mixed_copy(chunk, own_y, 1, True, 2).wait_recv()
        project(behind_y, chunk)
        mixed_copy(chunk, own_y, 0, False, 3).wait_recv()
        project(ahead_y, chunk)
        for copy in relay_copies(chunk):
            copy.wait_recv()
        project(across_y, chunk)

    def gather(chunk):
        pltpu.make_async_copy(
            conv_got.at[chunk], conv_got.at[chunk], conv_recv_sem.at[chunk]
        ).wait()
        for row in range(per_part):
            rows = pl.ds(pl.multiple_of(chunk * chunk_channels, chunk_channels), chunk_channels)
            columns = pl.ds(row * LANES, LANES)
            mixed[own_y, chunk, :, columns] = (
                conv_got[chunk, pl.ds(row, chunk_channels, stride=per_part), :]
                * query_t[rows, columns]
            )
        for copy in own_copies(chunk):
            copy.start()

    @pl.loop(0, CHUNKS + LAG)
    def _(step):
        @pl.when(step < CHUNKS)
        def _():
            convolve_chunk(step)

        @pl.when((step < CHUNKS) & (step > LAG))
        def _():
            relay(step - LAG - 1)

        @pl.when(step >= LAG)
        def _():
            gather(step - LAG)

        @pl.when(step == LAG)
        def _():
            prepare_weights()

        @pl.when((step >= CHUNKS) & (step > LAG))
        def _():
            relay(step - LAG - 1)

        @pl.when(step >= LAG)
        def _():
            project(own_y, step - LAG)

        @pl.when(step > LAG + 1)
        def _():
            finish(step - LAG - 2)

    relay(CHUNKS - 1)
    finish(CHUNKS - 2)
    finish(CHUNKS - 1)

    to_partner = pltpu.make_async_remote_copy(
        src_ref=total.at[pl.ds(partner_half, outs // 2), :],
        dst_ref=partner_got,
        send_sem=partner_send_sem,
        recv_sem=partner_recv_sem,
        device_id={"ch": partner},
        device_id_type=MESH,
    )
    to_partner.start()

    @pl.loop(0, CHUNKS)
    def _(chunk):
        for which in range(2):
            rest_of = got.at[which, chunk, pl.ds(0, parts - 1)]
            pltpu.make_async_copy(rest_of, rest_of, send_sem.at[which, chunk]).wait()
        rest_of = conv_sent.at[chunk, pl.ds(0, parts - 1)]
        pltpu.make_async_copy(rest_of, rest_of, conv_send_sem.at[chunk]).wait()
        for copy in own_copies(chunk) + relay_copies(chunk):
            copy.wait_send()

    for step in range(1, ys):
        weight_copy(step).wait_send()
    to_partner.wait()
    out_ref[...] = total[pl.ds(own_half, outs // 2), :] + partner_got[...]


def per_device(query_rows, key_rows, value_rows, filters, skip_gain, out_weight):
    parts = lax.axis_size("seq")
    ys = lax.axis_size("ch") // 2
    length, channels = query_rows.shape
    per_part = length // LANES
    outs = out_weight.shape[1] // ys
    chunk_channels = channels // CHUNKS
    slab = chunk_channels // parts * per_part
    consts = tables(parts, per_part)
    f32 = jnp.float32
    dma = pltpu.SemaphoreType.DMA
    return pl.pallas_call(
        functools.partial(kernel, parts, ys),
        out_shape=pltpu.VMEM((outs // 2, length), f32),
        in_specs=[pl.BlockSpec(memory_space=pl.ANY)] * (6 + len(consts)),
        out_specs=pl.BlockSpec(memory_space=pltpu.VMEM),
        scratch_shapes=[
            *[pltpu.VMEM(table.shape, table.dtype) for table in consts],
            pltpu.VMEM((length, channels), f32),
            pltpu.VMEM((length, channels), f32),
            pltpu.VMEM((length, channels), f32),
            pltpu.VMEM((length, channels), f32),
            pltpu.VMEM((1, channels), f32),
            pltpu.VMEM((channels, length), f32),
            pltpu.VMEM((2, channels * per_part, LANES), f32),
            pltpu.VMEM((2, CHUNKS, parts, slab, LANES), f32),
            pltpu.VMEM((CHUNKS, parts, slab, LANES), f32),
            pltpu.VMEM((CHUNKS, parts * slab, LANES), f32),
            pltpu.VMEM((ys, channels, outs), f32),
            pltpu.VMEM((ys, CHUNKS, outs, 3 * chunk_channels), jnp.bfloat16),
            pltpu.VMEM((ys, CHUNKS, chunk_channels, length), f32),
            pltpu.VMEM((outs, length), f32),
            pltpu.VMEM((outs // 2, length), f32),
            dma((5,)),
            dma((len(consts),)),
            dma((2, CHUNKS)),
            dma((2, CHUNKS)),
            dma((CHUNKS,)),
            dma((CHUNKS,)),
            dma((ys - 1,)),
            dma((ys,)),
            dma((CHUNKS, 6)),
            dma((CHUNKS, 6)),
            dma(()),
            dma(()),
        ],
        compiler_params=pltpu.CompilerParams(collective_id=0, has_side_effects=True),
    )(
        query_rows,
        key_rows,
        value_rows,
        filters,
        skip_gain.reshape(1, channels),
        out_weight,
        *[jnp.asarray(table) for table in consts],
    )


def solution(mesh):
    in_specs = (
        P("seq", "ch"),
        P("seq", "ch"),
        P("seq", "ch"),
        P("seq", "ch"),
        P("ch"),
        P("ch", None),
    )
    out_specs = P("ch", "seq")
    return jax.shard_map(
        per_device, mesh=mesh, in_specs=in_specs, out_specs=out_specs, check_vma=False
    )
```

```python
import functools
import math

import jax
import jax.numpy as jnp
import numpy as np
from jax import lax
from jax.experimental import pallas as pl
from jax.experimental.pallas import tpu as pltpu
from jax.sharding import PartitionSpec as P

CHUNKS = 4
HELD = 1
LAG = CHUNKS - 1 - HELD
LANES = 128
MESH = pl.DeviceIdType.MESH


def split_table(table):
    high = table.astype(jnp.bfloat16)
    low = (table - high.astype(np.float64)).astype(jnp.bfloat16)
    return high, low


def tables(parts, per_part):
    rows = parts * per_part
    period = 2 * rows * LANES
    odd = np.arange(rows) + 0.5
    outer = 2 * math.pi * odd[:, None] * np.arange(rows)[None, :] / (2 * rows)
    first = np.zeros((2, 2, rows, parts, 2, per_part))
    for pair in range(2):
        first[0, pair, :, :, pair, :] = np.cos(outer).reshape(rows, parts, per_part)
        first[1, pair, :, :, pair, :] = -np.sin(outer).reshape(rows, parts, per_part)
    first = first.reshape(4 * rows, 2 * rows)
    last = first.T * (2.0 / period)
    turn = 2 * math.pi * odd[:, None] * np.arange(LANES)[None, :] / period
    turn_cos = np.tile(np.cos(turn), (2, 1)).astype(np.float32)
    turn_sin = np.tile(np.sin(turn), (2, 1)).astype(np.float32)
    inner = 2 * math.pi * (np.arange(LANES)[:, None] * np.arange(LANES)[None, :] % LANES) / LANES
    cos, sin = np.cos(inner), np.sin(inner)
    ahead = np.block([[cos, -sin], [sin, cos]])
    behind = np.block([[cos, sin], [-sin, cos]])
    return (
        *split_table(first),
        *split_table(last),
        *split_table(ahead),
        *split_table(behind),
        turn_cos,
        turn_sin,
    )


def split(value):
    high = value.astype(jnp.bfloat16)
    low = (value - high.astype(jnp.float32)).astype(jnp.bfloat16)
    return high, low


def dot(a, b):
    return jnp.dot(a, b, preferred_element_type=jnp.float32)


def dot3(a, b):
    return dot(a[0], b[0]) + dot(a[0], b[1]) + dot(a[1], b[0])


def dot3_narrow(a, b):
    width = b[0].shape[1]
    both = dot(a[0], jnp.concatenate(b, axis=1))
    return both[:, :width] + both[:, width:] + dot(a[1], b[0])


def spectrum(data, first, ahead, cos, sin):
    half = data.shape[0]
    stage = dot3_narrow(first, split(data))
    re, im = stage[:half], stage[half:]
    stage = jnp.concatenate([re * cos + im * sin, im * cos - re * sin], axis=1)
    return dot3(split(stage), ahead)


def inverse(product, behind, last, cos, sin):
    stage = dot3(split(product), behind)
    re, im = stage[:, :LANES], stage[:, LANES:]
    stage = jnp.concatenate([re * cos - im * sin, im * cos + re * sin], axis=0)
    return dot3_narrow(last, split(stage))


def kernel(
    parts,
    ys,
    query_hbm,
    key_hbm,
    value_hbm,
    filter_hbm,
    skip_hbm,
    weight_hbm,
    *rest,
):
    table_hbm, rest = rest[:10], rest[10:]
    out_ref, rest = rest[0], rest[1:]
    table_ref, rest = rest[:10], rest[10:]
    (
        query_in,
        key_in,
        value_in,
        filter_in,
        skip_in,
        query_t,
        filter_spectrum,
        sent,
        got,
        conv_sent,
        conv_got,
        weights,
        weight_t,
        mixed,
        total,
        partner_got,
        load_sem,
        table_sem,
        send_sem,
        recv_sem,
        conv_send_sem,
        conv_recv_sem,
        weight_send_sem,
        weight_recv_sem,
        mixed_send_sem,
        mixed_recv_sem,
        partner_send_sem,
        partner_recv_sem,
    ) = rest
    length, channels = query_in.shape
    per_part = length // LANES
    chunk_channels = channels // CHUNKS
    slab = chunk_channels // parts * per_part
    outs = weights.shape[2]
    me = lax.axis_index("seq")
    lane = lax.axis_index("ch")
    core = lax.rem(lane, 2)
    own_y = lane // 2
    partner = lane + 1 - 2 * core
    own_half = pl.multiple_of(core * (outs // 2), outs // 2)
    partner_half = pl.multiple_of((1 - core) * (outs // 2), outs // 2)

    loads = [
        pltpu.make_async_copy(source, target, load_sem.at[number])
        for number, (source, target) in enumerate(
            [
                (filter_hbm, filter_in),
                (skip_hbm, skip_in),
                (key_hbm, key_in),
                (value_hbm, value_in),
                (query_hbm, query_in),
            ]
        )
    ]
    for load in loads[:4]:
        load.start()

    barrier = pltpu.get_barrier_semaphore()

    @pl.loop(1, parts)
    def _(step):
        pl.semaphore_signal(
            barrier, inc=1, device_id={"seq": lax.rem(me + step, parts)}, device_id_type=MESH
        )

    @pl.loop(1, ys)
    def _(step):
        pl.semaphore_signal(
            barrier, inc=1, device_id={"ch": lax.rem(lane + 2 * step, 2 * ys)}, device_id_type=MESH
        )

    pl.semaphore_signal(barrier, inc=1, device_id={"ch": partner}, device_id_type=MESH)

    loads[4].start()
    table_loads = [
        pltpu.make_async_copy(source, target, table_sem.at[number])
        for number, (source, target) in enumerate(zip(table_hbm, table_ref))
    ]
    for load in table_loads:
        load.start()

    def place(source, which, columns):
        for row in range(per_part):
            block = source(pl.ds(row * LANES, LANES), pl.ds(columns, LANES))
            sent[which, pl.ds(columns * per_part + row, LANES, stride=per_part), :] = block.T

    for load in loads[:4]:
        load.wait()
    tap = jnp.where(me == 0, 1.0, 0.0).astype(jnp.float32)
    filter_in[0:1, :] = filter_in[0:1, :] + tap * skip_in[...]

    def send_chunk(chunk):
        for which in (1, 0):

            @pl.loop(1, parts)
            def _(step):
                peer = lax.rem(me + step, parts)
                start = pl.multiple_of(chunk * parts * slab + peer * slab, slab)
                pltpu.make_async_remote_copy(
                    src_ref=sent.at[which, pl.ds(start, slab), :],
                    dst_ref=got.at[which, chunk, me],
                    send_sem=send_sem.at[which, chunk],
                    recv_sem=recv_sem.at[which, chunk],
                    device_id={"seq": peer},
                    device_id_type=MESH,
                ).start()

            start = pl.multiple_of(chunk * parts * slab + me * slab, slab)
            pltpu.make_async_copy(
                sent.at[which, pl.ds(start, slab), :],
                got.at[which, chunk, me],
                recv_sem.at[which, chunk],
            ).start()

    def gated(rows, columns):
        return key_in[rows, columns] * value_in[rows, columns]

    def plain(rows, columns):
        return filter_in[rows, columns]

    def weight_copy(step):
        peer_y = lax.rem(own_y + step, ys)
        start = pl.multiple_of(peer_y * outs, outs)
        return pltpu.make_async_remote_copy(
            src_ref=weight_hbm.at[:, pl.ds(start, outs)],
            dst_ref=weights.at[own_y],
            send_sem=weight_send_sem.at[step - 1],
            recv_sem=weight_recv_sem.at[step - 1],
            device_id={"ch": lax.rem(lane + 2 * step, 2 * ys)},
            device_id_type=MESH,
        )

    own_weight = pltpu.make_async_copy(
        weight_hbm.at[:, pl.ds(pl.multiple_of(own_y * outs, outs), outs)],
        weights.at[own_y],
        weight_recv_sem.at[ys - 1],
    )
    sent_chunks = 0
    for columns in range(0, channels, LANES):
        place(plain, 1, columns)
        place(gated, 0, columns)
        if columns == 0:
            pl.semaphore_wait(barrier, parts - 1 + ys - 1 + 1)
            for step in range(1, ys):
                weight_copy(step).start()
            own_weight.start()
        while (sent_chunks + 1) * chunk_channels <= columns + LANES:
            if sent_chunks < CHUNKS - HELD:
                send_chunk(sent_chunks)
            sent_chunks += 1

    loads[4].wait()
    for columns in range(0, channels, LANES):
        for row in range(per_part):
            query_t[pl.ds(columns, LANES), pl.ds(row * LANES, LANES)] = query_in[
                pl.ds(row * LANES, LANES), pl.ds(columns, LANES)
            ].T
    for load in table_loads:
        load.wait()

    first, last, ahead, behind = (
        (table_ref[2 * n][...], table_ref[2 * n + 1][...]) for n in range(4)
    )
    turn_cos, turn_sin = table_ref[8], table_ref[9]

    def prepare_weights():
        own_weight.wait()
        for step in range(1, ys):
            weight_copy(step).wait_recv()

        @pl.loop(0, ys)
        def _(y):
            for chunk in range(CHUNKS):
                for out in range(0, outs, LANES):
                    block = weights[y, pl.ds(chunk * chunk_channels, chunk_channels), pl.ds(out, LANES)].T
                    high, low = split(block)
                    weight_t[y, chunk, pl.ds(out, LANES), :] = jnp.concatenate([high, low, high], axis=1)

    def convolve_chunk(chunk):
        def arrived(which):
            pltpu.make_async_copy(
                got.at[which, chunk], got.at[which, chunk], recv_sem.at[which, chunk]
            ).wait()

        def transformed(which, rows):
            data = got[which, chunk, :, rows, :].reshape(parts * 8, LANES)
            return spectrum(data, first, ahead, turn_cos[...], turn_sin[...])

        arrived(1)

        @pl.loop(0, slab // 8)
        def _(pair):
            rows = pl.ds(pl.multiple_of(pair * 8, 8), 8)
            filter_spectrum[pair] = transformed(1, rows)

        arrived(0)

        @pl.loop(0, slab // 8)
        def _(pair):
            rows = pl.ds(pl.multiple_of(pair * 8, 8), 8)
            stage = transformed(0, rows)
            gre, gim = stage[:, :LANES], stage[:, LANES:]
            fre, fim = filter_spectrum[pair, :, :LANES], filter_spectrum[pair, :, LANES:]
            product = jnp.concatenate([gre * fre - gim * fim, gre * fim + gim * fre], axis=1)
            done = inverse(product, behind, last, turn_cos[...], turn_sin[...])
            conv_sent[chunk, :, rows, :] = done.reshape(parts, 8, LANES)

        place_at = pl.ds(pl.multiple_of(me * slab, slab), slab)

        @pl.loop(1, parts)
        def _(step):
            peer = lax.rem(me + step, parts)
            pltpu.make_async_remote_copy(
                src_ref=conv_sent.at[chunk, peer],
                dst_ref=conv_got.at[chunk, place_at, :],
                send_sem=conv_send_sem.at[chunk],
                recv_sem=conv_recv_sem.at[chunk],
                device_id={"seq": peer},
                device_id_type=MESH,
            ).start()

        pltpu.make_async_copy(
            conv_sent.at[chunk, me], conv_got.at[chunk, place_at, :], conv_recv_sem.at[chunk]
        ).start()

        @pl.when(chunk < HELD)
        def _():
            send_chunk(chunk + CHUNKS - HELD)

    total[...] = jnp.zeros_like(total)

    ahead_y, behind_y = lax.rem(own_y + 1, ys), lax.rem(own_y + ys - 1, ys)
    across_y = lax.rem(own_y + 2, ys)
    half_rows = chunk_channels // 2

    def mixed_copy(chunk, owner, half, up, slot):
        return pltpu.make_async_remote_copy(
            src_ref=mixed.at[owner, chunk, pl.ds(half * half_rows, half_rows), :],
            dst_ref=mixed.at[owner, chunk, pl.ds(half * half_rows, half_rows), :],
            send_sem=mixed_send_sem.at[chunk, slot],
            recv_sem=mixed_recv_sem.at[chunk, slot],
            device_id={"ch": lax.rem(lane + (2 if up else 2 * ys - 2), 2 * ys)},
            device_id_type=MESH,
        )

    def own_copies(chunk):
        return [
            mixed_copy(chunk, own_y, 0, True, 0),
            mixed_copy(chunk, own_y, 1, False, 1),
            mixed_copy(chunk, own_y, 1, True, 2),
            mixed_copy(chunk, own_y, 0, False, 3),
        ]

    def relay_copies(chunk):
        return [
            mixed_copy(chunk, behind_y, 0, True, 4),
            mixed_copy(chunk, ahead_y, 1, False, 5),
        ]

    def project(y, chunk):
        high, low = split(mixed[y, chunk])
        data = jnp.concatenate([high, high, low], axis=0)
        total[...] += dot(weight_t[y, chunk], data)

    def relay(chunk):
        mixed_copy(chunk, own_y, 0, True, 0).wait_recv()
        mixed_copy(chunk, behind_y, 0, True, 4).start()
        mixed_copy(chunk, own_y, 1, False, 1).wait_recv()
        mixed_copy(chunk, ahead_y, 1, False, 5).start()

    to_partner = pltpu.make_async_remote_copy(
        src_ref=total.at[pl.ds(partner_half, outs // 2), :],
        dst_ref=partner_got,
        send_sem=partner_send_sem,
        recv_sem=partner_recv_sem,
        device_id={"ch": partner},
        device_id_type=MESH,
    )

    def finish(chunk, final=False):
        mixed_copy(chunk, own_y, 1, True, 2).wait_recv()
        project(behind_y, chunk)
        mixed_copy(chunk, own_y, 0, False, 3).wait_recv()
        project(ahead_y, chunk)
        for copy in relay_copies(chunk):
            copy.wait_recv()
        if not final:
            project(across_y, chunk)
            return
        high, low = split(mixed[across_y, chunk])
        data = jnp.concatenate([high, high, low], axis=0)
        for start in (partner_half, own_half):
            rows = pl.ds(start, outs // 2)
            total[rows, :] += dot(weight_t[across_y, chunk, rows, :], data)
            if start is partner_half:
                to_partner.start()

    def gather(chunk):
        pltpu.make_async_copy(
            conv_got.at[chunk], conv_got.at[chunk], conv_recv_sem.at[chunk]
        ).wait()
        for row in range(per_part):
            rows = pl.ds(pl.multiple_of(chunk * chunk_channels, chunk_channels), chunk_channels)
            columns = pl.ds(row * LANES, LANES)
            mixed[own_y, chunk, :, columns] = (
                conv_got[chunk, pl.ds(row, chunk_channels, stride=per_part), :]
                * query_t[rows, columns]
            )
        for copy in own_copies(chunk):
            copy.start()

    @pl.loop(0, CHUNKS + LAG)
    def _(step):
        @pl.when(step < CHUNKS)
        def _():
            convolve_chunk(step)

        @pl.when((step < CHUNKS) & (step > LAG))
        def _():
            relay(step - LAG - 1)

        @pl.when(step >= LAG)
        def _():
            gather(step - LAG)

        @pl.when(step == LAG)
        def _():
            prepare_weights()

        @pl.when((step >= CHUNKS) & (step > LAG))
        def _():
            relay(step - LAG - 1)

        @pl.when(step >= LAG)
        def _():
            project(own_y, step - LAG)

        @pl.when(step > LAG + 1)
        def _():
            finish(step - LAG - 2)

    relay(CHUNKS - 1)
    finish(CHUNKS - 2)
    finish(CHUNKS - 1, final=True)


    @pl.loop(0, CHUNKS)
    def _(chunk):
        for which in range(2):
            rest_of = got.at[which, chunk, pl.ds(0, parts - 1)]
            pltpu.make_async_copy(rest_of, rest_of, send_sem.at[which, chunk]).wait()
        rest_of = conv_sent.at[chunk, pl.ds(0, parts - 1)]
        pltpu.make_async_copy(rest_of, rest_of, conv_send_sem.at[chunk]).wait()
        for copy in own_copies(chunk) + relay_copies(chunk):
            copy.wait_send()

    for step in range(1, ys):
        weight_copy(step).wait_send()
    to_partner.wait()
    out_ref[...] = total[pl.ds(own_half, outs // 2), :] + partner_got[...]


def per_device(query_rows, key_rows, value_rows, filters, skip_gain, out_weight):
    parts = lax.axis_size("seq")
    ys = lax.axis_size("ch") // 2
    length, channels = query_rows.shape
    per_part = length // LANES
    outs = out_weight.shape[1] // ys
    chunk_channels = channels // CHUNKS
    slab = chunk_channels // parts * per_part
    consts = tables(parts, per_part)
    f32 = jnp.float32
    dma = pltpu.SemaphoreType.DMA
    return pl.pallas_call(
        functools.partial(kernel, parts, ys),
        out_shape=pltpu.VMEM((outs // 2, length), f32),
        in_specs=[pl.BlockSpec(memory_space=pl.ANY)] * (6 + len(consts)),
        out_specs=pl.BlockSpec(memory_space=pltpu.VMEM),
        scratch_shapes=[
            *[pltpu.VMEM(table.shape, table.dtype) for table in consts],
            pltpu.VMEM((length, channels), f32),
            pltpu.VMEM((length, channels), f32),
            pltpu.VMEM((length, channels), f32),
            pltpu.VMEM((length, channels), f32),
            pltpu.VMEM((1, channels), f32),
            pltpu.VMEM((channels, length), f32),
            pltpu.VMEM((slab // 8, 2 * parts * per_part, 2 * LANES), f32),
            pltpu.VMEM((2, channels * per_part, LANES), f32),
            pltpu.VMEM((2, CHUNKS, parts, slab, LANES), f32),
            pltpu.VMEM((CHUNKS, parts, slab, LANES), f32),
            pltpu.VMEM((CHUNKS, parts * slab, LANES), f32),
            pltpu.VMEM((ys, channels, outs), f32),
            pltpu.VMEM((ys, CHUNKS, outs, 3 * chunk_channels), jnp.bfloat16),
            pltpu.VMEM((ys, CHUNKS, chunk_channels, length), f32),
            pltpu.VMEM((outs, length), f32),
            pltpu.VMEM((outs // 2, length), f32),
            dma((5,)),
            dma((len(consts),)),
            dma((2, CHUNKS)),
            dma((2, CHUNKS)),
            dma((CHUNKS,)),
            dma((CHUNKS,)),
            dma((ys - 1,)),
            dma((ys,)),
            dma((CHUNKS, 6)),
            dma((CHUNKS, 6)),
            dma(()),
            dma(()),
        ],
        compiler_params=pltpu.CompilerParams(collective_id=0, has_side_effects=True),
    )(
        query_rows,
        key_rows,
        value_rows,
        filters,
        skip_gain.reshape(1, channels),
        out_weight,
        *[jnp.asarray(table) for table in consts],
    )


def solution(mesh):
    in_specs = (
        P("seq", "ch"),
        P("seq", "ch"),
        P("seq", "ch"),
        P("seq", "ch"),
        P("ch"),
        P("ch", None),
    )
    out_specs = P("ch", "seq")
    return jax.shard_map(
        per_device, mesh=mesh, in_specs=in_specs, out_specs=out_specs, check_vma=False
    )
```

```python
import functools
import math

import jax
import jax.numpy as jnp
import numpy as np
from jax import lax
from jax.experimental import pallas as pl
from jax.experimental.pallas import tpu as pltpu
from jax.sharding import PartitionSpec as P

CHUNKS = 4
HELD = 1
LAG = CHUNKS - 1 - HELD
LANES = 128
MESH = pl.DeviceIdType.MESH


def split_table(table):
    high = table.astype(jnp.bfloat16)
    low = (table - high.astype(np.float64)).astype(jnp.bfloat16)
    return high, low


def tables(parts, per_part):
    rows = parts * per_part
    period = 2 * rows * LANES
    odd = np.arange(rows) + 0.5
    outer = 2 * math.pi * odd[:, None] * np.arange(rows)[None, :] / (2 * rows)
    first = np.zeros((2, 2, rows, parts, 2, per_part))
    for pair in range(2):
        first[0, pair, :, :, pair, :] = np.cos(outer).reshape(rows, parts, per_part)
        first[1, pair, :, :, pair, :] = -np.sin(outer).reshape(rows, parts, per_part)
    first = first.reshape(4 * rows, 2 * rows)
    last = first.T * (2.0 / period)
    turn = 2 * math.pi * odd[:, None] * np.arange(LANES)[None, :] / period
    turn_cos = np.tile(np.cos(turn), (2, 1)).astype(np.float32)
    turn_sin = np.tile(np.sin(turn), (2, 1)).astype(np.float32)
    inner = 2 * math.pi * (np.arange(LANES)[:, None] * np.arange(LANES)[None, :] % LANES) / LANES
    cos, sin = np.cos(inner), np.sin(inner)
    ahead = np.block([[cos, -sin], [sin, cos]])
    behind = np.block([[cos, sin], [-sin, cos]])
    return (
        *split_table(first),
        *split_table(last),
        *split_table(ahead),
        *split_table(behind),
        turn_cos,
        turn_sin,
    )


def split(value):
    high = value.astype(jnp.bfloat16)
    low = (value - high.astype(jnp.float32)).astype(jnp.bfloat16)
    return high, low


def dot(a, b):
    return jnp.dot(a, b, preferred_element_type=jnp.float32)


def dot3(a, b):
    return dot(a[0], b[0]) + dot(a[0], b[1]) + dot(a[1], b[0])


def dot3_narrow(a, b):
    width = b[0].shape[1]
    both = dot(a[0], jnp.concatenate(b, axis=1))
    return both[:, :width] + both[:, width:] + dot(a[1], b[0])


def spectrum(data, first, ahead, cos, sin):
    half = data.shape[0]
    stage = dot3_narrow(first, split(data))
    re, im = stage[:half], stage[half:]
    stage = jnp.concatenate([re * cos + im * sin, im * cos - re * sin], axis=1)
    return dot3(split(stage), ahead)


def inverse(product, behind, last, cos, sin):
    stage = dot3(split(product), behind)
    re, im = stage[:, :LANES], stage[:, LANES:]
    stage = jnp.concatenate([re * cos - im * sin, im * cos + re * sin], axis=0)
    return dot3_narrow(last, split(stage))


def kernel(
    parts,
    ys,
    query_hbm,
    key_hbm,
    value_hbm,
    filter_hbm,
    skip_hbm,
    weight_hbm,
    *rest,
):
    table_hbm, rest = rest[:10], rest[10:]
    out_ref, partner_got, rest = rest[0], rest[1], rest[2:]
    table_ref, rest = rest[:10], rest[10:]
    (
        query_in,
        key_in,
        value_in,
        filter_in,
        skip_in,
        query_t,
        filter_spectrum,
        sent,
        got,
        conv_sent,
        conv_got,
        weights,
        weight_t,
        mixed,
        total,
        load_sem,
        table_sem,
        send_sem,
        recv_sem,
        conv_send_sem,
        conv_recv_sem,
        weight_send_sem,
        weight_recv_sem,
        mixed_send_sem,
        mixed_recv_sem,
        partner_send_sem,
        partner_recv_sem,
    ) = rest
    length, channels = query_in.shape
    per_part = length // LANES
    chunk_channels = channels // CHUNKS
    slab = chunk_channels // parts * per_part
    outs = weights.shape[2]
    me = lax.axis_index("seq")
    lane = lax.axis_index("ch")
    core = lax.rem(lane, 2)
    own_y = lane // 2
    partner = lane + 1 - 2 * core
    own_half = pl.multiple_of(core * (outs // 2), outs // 2)
    partner_half = pl.multiple_of((1 - core) * (outs // 2), outs // 2)

    loads = [
        pltpu.make_async_copy(source, target, load_sem.at[number])
        for number, (source, target) in enumerate(
            [
                (filter_hbm, filter_in),
                (skip_hbm, skip_in),
                (key_hbm, key_in),
                (value_hbm, value_in),
                (query_hbm, query_in),
            ]
        )
    ]
    for load in loads[:4]:
        load.start()

    barrier = pltpu.get_barrier_semaphore()

    @pl.loop(1, parts)
    def _(step):
        pl.semaphore_signal(
            barrier, inc=1, device_id={"seq": lax.rem(me + step, parts)}, device_id_type=MESH
        )

    @pl.loop(1, ys)
    def _(step):
        pl.semaphore_signal(
            barrier, inc=1, device_id={"ch": lax.rem(lane + 2 * step, 2 * ys)}, device_id_type=MESH
        )

    pl.semaphore_signal(barrier, inc=1, device_id={"ch": partner}, device_id_type=MESH)

    loads[4].start()
    table_loads = [
        pltpu.make_async_copy(source, target, table_sem.at[number])
        for number, (source, target) in enumerate(zip(table_hbm, table_ref))
    ]
    for load in table_loads:
        load.start()

    def place(source, which, columns):
        for row in range(per_part):
            block = source(pl.ds(row * LANES, LANES), pl.ds(columns, LANES))
            sent[which, pl.ds(columns * per_part + row, LANES, stride=per_part), :] = block.T

    for load in loads[:4]:
        load.wait()
    tap = jnp.where(me == 0, 1.0, 0.0).astype(jnp.float32)
    filter_in[0:1, :] = filter_in[0:1, :] + tap * skip_in[...]

    def send_chunk(chunk):
        def slab_of(peer):
            start = pl.multiple_of(chunk * parts * slab + peer * slab, slab)
            return sent.at[:, pl.ds(start, slab), :]

        @pl.loop(1, parts)
        def _(step):
            peer = lax.rem(me + step, parts)
            pltpu.make_async_remote_copy(
                src_ref=slab_of(peer),
                dst_ref=got.at[:, chunk, me],
                send_sem=send_sem.at[0, chunk],
                recv_sem=recv_sem.at[0, chunk],
                device_id={"seq": peer},
                device_id_type=MESH,
            ).start()

        pltpu.make_async_copy(slab_of(me), got.at[:, chunk, me], recv_sem.at[0, chunk]).start()

    def gated(rows, columns):
        return key_in[rows, columns] * value_in[rows, columns]

    def plain(rows, columns):
        return filter_in[rows, columns]

    def weight_copy(step):
        peer_y = lax.rem(own_y + step, ys)
        start = pl.multiple_of(peer_y * outs, outs)
        return pltpu.make_async_remote_copy(
            src_ref=weight_hbm.at[:, pl.ds(start, outs)],
            dst_ref=weights.at[own_y],
            send_sem=weight_send_sem.at[step - 1],
            recv_sem=weight_recv_sem.at[step - 1],
            device_id={"ch": lax.rem(lane + 2 * step, 2 * ys)},
            device_id_type=MESH,
        )

    own_weight = pltpu.make_async_copy(
        weight_hbm.at[:, pl.ds(pl.multiple_of(own_y * outs, outs), outs)],
        weights.at[own_y],
        weight_recv_sem.at[ys - 1],
    )
    sent_chunks = 0
    for columns in range(0, channels, LANES):
        place(plain, 1, columns)
        place(gated, 0, columns)
        if columns == 0:
            pl.semaphore_wait(barrier, parts - 1 + ys - 1 + 1)
            for step in range(1, ys):
                weight_copy(step).start()
            own_weight.start()
        while (sent_chunks + 1) * chunk_channels <= columns + LANES:
            if sent_chunks < CHUNKS - HELD:
                send_chunk(sent_chunks)
            sent_chunks += 1

    loads[4].wait()
    for columns in range(0, channels, LANES):
        for row in range(per_part):
            query_t[pl.ds(columns, LANES), pl.ds(row * LANES, LANES)] = query_in[
                pl.ds(row * LANES, LANES), pl.ds(columns, LANES)
            ].T
    for load in table_loads:
        load.wait()

    first, last, ahead, behind = (
        (table_ref[2 * n][...], table_ref[2 * n + 1][...]) for n in range(4)
    )
    turn_cos, turn_sin = table_ref[8], table_ref[9]

    def prepare_weights():
        own_weight.wait()
        for step in range(1, ys):
            weight_copy(step).wait_recv()

        @pl.loop(0, ys)
        def _(y):
            for chunk in range(CHUNKS):
                for out in range(0, outs, LANES):
                    block = weights[y, pl.ds(chunk * chunk_channels, chunk_channels), pl.ds(out, LANES)].T
                    high, low = split(block)
                    weight_t[y, chunk, pl.ds(out, LANES), :] = jnp.concatenate([high, low, high], axis=1)

    def convolve_chunk(chunk):
        def arrived(which):
            pltpu.make_async_copy(
                got.at[which, chunk], got.at[which, chunk], recv_sem.at[which, chunk]
            ).wait()

        def transformed(which, rows):
            data = got[which, chunk, :, rows, :].reshape(parts * 8, LANES)
            return spectrum(data, first, ahead, turn_cos[...], turn_sin[...])

        both = got.at[:, chunk]
        pltpu.make_async_copy(both, both, recv_sem.at[0, chunk]).wait()

        @pl.loop(0, slab // 8)
        def _(pair):
            rows = pl.ds(pl.multiple_of(pair * 8, 8), 8)
            filter_spectrum[pair] = transformed(1, rows)


        @pl.loop(0, slab // 8)
        def _(pair):
            rows = pl.ds(pl.multiple_of(pair * 8, 8), 8)
            stage = transformed(0, rows)
            gre, gim = stage[:, :LANES], stage[:, LANES:]
            fre, fim = filter_spectrum[pair, :, :LANES], filter_spectrum[pair, :, LANES:]
            product = jnp.concatenate([gre * fre - gim * fim, gre * fim + gim * fre], axis=1)
            done = inverse(product, behind, last, turn_cos[...], turn_sin[...])
            conv_sent[chunk, :, rows, :] = done.reshape(parts, 8, LANES)

        place_at = pl.ds(pl.multiple_of(me * slab, slab), slab)

        @pl.loop(1, parts)
        def _(step):
            peer = lax.rem(me + step, parts)
            pltpu.make_async_remote_copy(
                src_ref=conv_sent.at[chunk, peer],
                dst_ref=conv_got.at[chunk, place_at, :],
                send_sem=conv_send_sem.at[chunk],
                recv_sem=conv_recv_sem.at[chunk],
                device_id={"seq": peer},
                device_id_type=MESH,
            ).start()

        pltpu.make_async_copy(
            conv_sent.at[chunk, me], conv_got.at[chunk, place_at, :], conv_recv_sem.at[chunk]
        ).start()

        @pl.when(chunk < HELD)
        def _():
            send_chunk(chunk + CHUNKS - HELD)

    total[...] = jnp.zeros_like(total)

    ahead_y, behind_y = lax.rem(own_y + 1, ys), lax.rem(own_y + ys - 1, ys)
    across_y = lax.rem(own_y + 2, ys)
    half_rows = chunk_channels // 2

    def mixed_copy(chunk, owner, half, up, slot):
        return pltpu.make_async_remote_copy(
            src_ref=mixed.at[owner, chunk, pl.ds(half * half_rows, half_rows), :],
            dst_ref=mixed.at[owner, chunk, pl.ds(half * half_rows, half_rows), :],
            send_sem=mixed_send_sem.at[chunk, slot],
            recv_sem=mixed_recv_sem.at[chunk, slot],
            device_id={"ch": lax.rem(lane + (2 if up else 2 * ys - 2), 2 * ys)},
            device_id_type=MESH,
        )

    def own_copies(chunk):
        return [
            mixed_copy(chunk, own_y, 0, True, 0),
            mixed_copy(chunk, own_y, 1, False, 1),
            mixed_copy(chunk, own_y, 1, True, 2),
            mixed_copy(chunk, own_y, 0, False, 3),
        ]

    def relay_copies(chunk):
        return [
            mixed_copy(chunk, behind_y, 0, True, 4),
            mixed_copy(chunk, ahead_y, 1, False, 5),
        ]

    def project(y, chunk):
        high, low = split(mixed[y, chunk])
        data = jnp.concatenate([high, high, low], axis=0)
        total[...] += dot(weight_t[y, chunk], data)

    def relay(chunk):
        mixed_copy(chunk, own_y, 0, True, 0).wait_recv()
        mixed_copy(chunk, behind_y, 0, True, 4).start()
        mixed_copy(chunk, own_y, 1, False, 1).wait_recv()
        mixed_copy(chunk, ahead_y, 1, False, 5).start()

    to_partner = pltpu.make_async_remote_copy(
        src_ref=total.at[pl.ds(partner_half, outs // 2), :],
        dst_ref=partner_got,
        send_sem=partner_send_sem,
        recv_sem=partner_recv_sem,
        device_id={"ch": partner},
        device_id_type=MESH,
    )

    def finish(chunk, final=False):
        mixed_copy(chunk, own_y, 1, True, 2).wait_recv()
        project(behind_y, chunk)
        mixed_copy(chunk, own_y, 0, False, 3).wait_recv()
        project(ahead_y, chunk)
        for copy in relay_copies(chunk):
            copy.wait_recv()
        if not final:
            project(across_y, chunk)
            return
        high, low = split(mixed[across_y, chunk])
        data = jnp.concatenate([high, high, low], axis=0)
        rows = pl.ds(partner_half, outs // 2)
        total[rows, :] += dot(weight_t[across_y, chunk, rows, :], data)
        to_partner.start()
        rows = pl.ds(own_half, outs // 2)
        out_ref[...] = total[rows, :] + dot(weight_t[across_y, chunk, rows, :], data)

    def gather(chunk):
        pltpu.make_async_copy(
            conv_got.at[chunk], conv_got.at[chunk], conv_recv_sem.at[chunk]
        ).wait()
        for row in range(per_part):
            rows = pl.ds(pl.multiple_of(chunk * chunk_channels, chunk_channels), chunk_channels)
            columns = pl.ds(row * LANES, LANES)
            mixed[own_y, chunk, :, columns] = (
                conv_got[chunk, pl.ds(row, chunk_channels, stride=per_part), :]
                * query_t[rows, columns]
            )
        for copy in own_copies(chunk):
            copy.start()

    @pl.loop(0, CHUNKS + LAG)
    def _(step):
        @pl.when(step < CHUNKS)
        def _():
            convolve_chunk(step)

        @pl.when((step < CHUNKS) & (step > LAG))
        def _():
            relay(step - LAG - 1)

        @pl.when(step >= LAG)
        def _():
            gather(step - LAG)

        @pl.when(step == LAG)
        def _():
            prepare_weights()

        @pl.when((step >= CHUNKS) & (step > LAG))
        def _():
            relay(step - LAG - 1)

        @pl.when(step >= LAG)
        def _():
            project(own_y, step - LAG)

        @pl.when(step > LAG + 1)
        def _():
            finish(step - LAG - 2)

    relay(CHUNKS - 1)
    finish(CHUNKS - 2)
    finish(CHUNKS - 1, final=True)


    @pl.loop(0, CHUNKS)
    def _(chunk):
        rest_of = got.at[:, chunk, pl.ds(0, parts - 1)]
        pltpu.make_async_copy(rest_of, rest_of, send_sem.at[0, chunk]).wait()
        rest_of = conv_sent.at[chunk, pl.ds(0, parts - 1)]
        pltpu.make_async_copy(rest_of, rest_of, conv_send_sem.at[chunk]).wait()
        for copy in own_copies(chunk) + relay_copies(chunk):
            copy.wait_send()

    for step in range(1, ys):
        weight_copy(step).wait_send()
    to_partner.wait()


def per_device(query_rows, key_rows, value_rows, filters, skip_gain, out_weight):
    parts = lax.axis_size("seq")
    ys = lax.axis_size("ch") // 2
    length, channels = query_rows.shape
    per_part = length // LANES
    outs = out_weight.shape[1] // ys
    chunk_channels = channels // CHUNKS
    slab = chunk_channels // parts * per_part
    consts = tables(parts, per_part)
    f32 = jnp.float32
    dma = pltpu.SemaphoreType.DMA
    own, other = pl.pallas_call(
        functools.partial(kernel, parts, ys),
        out_shape=[pltpu.VMEM((outs // 2, length), f32)] * 2,
        in_specs=[pl.BlockSpec(memory_space=pl.ANY)] * (6 + len(consts)),
        out_specs=[pl.BlockSpec(memory_space=pltpu.VMEM)] * 2,
        scratch_shapes=[
            *[pltpu.VMEM(table.shape, table.dtype) for table in consts],
            pltpu.VMEM((length, channels), f32),
            pltpu.VMEM((length, channels), f32),
            pltpu.VMEM((length, channels), f32),
            pltpu.VMEM((length, channels), f32),
            pltpu.VMEM((1, channels), f32),
            pltpu.VMEM((channels, length), f32),
            pltpu.VMEM((slab // 8, 2 * parts * per_part, 2 * LANES), f32),
            pltpu.VMEM((2, channels * per_part, LANES), f32),
            pltpu.VMEM((2, CHUNKS, parts, slab, LANES), f32),
            pltpu.VMEM((CHUNKS, parts, slab, LANES), f32),
            pltpu.VMEM((CHUNKS, parts * slab, LANES), f32),
            pltpu.VMEM((ys, channels, outs), f32),
            pltpu.VMEM((ys, CHUNKS, outs, 3 * chunk_channels), jnp.bfloat16),
            pltpu.VMEM((ys, CHUNKS, chunk_channels, length), f32),
            pltpu.VMEM((outs, length), f32),
            dma((5,)),
            dma((len(consts),)),
            dma((2, CHUNKS)),
            dma((2, CHUNKS)),
            dma((CHUNKS,)),
            dma((CHUNKS,)),
            dma((ys - 1,)),
            dma((ys,)),
            dma((CHUNKS, 6)),
            dma((CHUNKS, 6)),
            dma(()),
            dma(()),
        ],
        compiler_params=pltpu.CompilerParams(collective_id=0, has_side_effects=True),
    )(
        query_rows,
        key_rows,
        value_rows,
        filters,
        skip_gain.reshape(1, channels),
        out_weight,
        *[jnp.asarray(table) for table in consts],
    )
    return own + other


def solution(mesh):
    in_specs = (
        P("seq", "ch"),
        P("seq", "ch"),
        P("seq", "ch"),
        P("seq", "ch"),
        P("ch"),
        P("ch", None),
    )
    out_specs = P("ch", "seq")
    return jax.shard_map(
        per_device, mesh=mesh, in_specs=in_specs, out_specs=out_specs, check_vma=False
    )
```

```python
import functools
import math

import jax
import jax.numpy as jnp
import numpy as np
from jax import lax
from jax.experimental import pallas as pl
from jax.experimental.pallas import tpu as pltpu
from jax.sharding import PartitionSpec as P

CHUNKS = 4
HELD = 1
LAG = CHUNKS - 1 - HELD
LANES = 128
MESH = pl.DeviceIdType.MESH


def split_table(table):
    high = table.astype(jnp.bfloat16)
    low = (table - high.astype(np.float64)).astype(jnp.bfloat16)
    return high, low


def tables(parts, per_part):
    rows = parts * per_part
    period = 2 * rows * LANES
    odd = np.arange(rows) + 0.5
    outer = 2 * math.pi * odd[:, None] * np.arange(rows)[None, :] / (2 * rows)
    first = np.zeros((2, 2, rows, parts, 2, per_part))
    for pair in range(2):
        first[0, pair, :, :, pair, :] = np.cos(outer).reshape(rows, parts, per_part)
        first[1, pair, :, :, pair, :] = -np.sin(outer).reshape(rows, parts, per_part)
    first = first.reshape(4 * rows, 2 * rows)
    last = first.T * (2.0 / period)
    turn = 2 * math.pi * odd[:, None] * np.arange(LANES)[None, :] / period
    turn_cos = np.tile(np.cos(turn), (2, 1)).astype(np.float32)
    turn_sin = np.tile(np.sin(turn), (2, 1)).astype(np.float32)
    inner = 2 * math.pi * (np.arange(LANES)[:, None] * np.arange(LANES)[None, :] % LANES) / LANES
    cos, sin = np.cos(inner), np.sin(inner)
    ahead = np.block([[cos, -sin], [sin, cos]])
    behind = np.block([[cos, sin], [-sin, cos]])
    return (
        *split_table(first),
        *split_table(last),
        *split_table(ahead),
        *split_table(behind),
        turn_cos,
        turn_sin,
    )


def split(value):
    high = value.astype(jnp.bfloat16)
    low = (value - high.astype(jnp.float32)).astype(jnp.bfloat16)
    return high, low


def dot(a, b):
    return jnp.dot(a, b, preferred_element_type=jnp.float32)


def dot3(a, b):
    return dot(a[0], b[0]) + dot(a[0], b[1]) + dot(a[1], b[0])


def dot3_narrow(a, b):
    width = b[0].shape[1]
    both = dot(a[0], jnp.concatenate(b, axis=1))
    return both[:, :width] + both[:, width:] + dot(a[1], b[0])


def spectrum(data, first, ahead, cos, sin):
    half = data.shape[0]
    stage = dot3_narrow(first, split(data))
    re, im = stage[:half], stage[half:]
    stage = jnp.concatenate([re * cos + im * sin, im * cos - re * sin], axis=1)
    return dot3(split(stage), ahead)


def inverse(product, behind, last, cos, sin):
    stage = dot3(split(product), behind)
    re, im = stage[:, :LANES], stage[:, LANES:]
    stage = jnp.concatenate([re * cos - im * sin, im * cos + re * sin], axis=0)
    return dot3_narrow(last, split(stage))


def kernel(
    parts,
    ys,
    query_hbm,
    key_hbm,
    value_hbm,
    filter_hbm,
    skip_hbm,
    weight_hbm,
    *rest,
):
    table_hbm, rest = rest[:10], rest[10:]
    out_ref, partner_got, rest = rest[0], rest[1], rest[2:]
    table_ref, rest = rest[:10], rest[10:]
    (
        query_in,
        key_in,
        value_in,
        filter_in,
        skip_in,
        query_t,
        filter_spectrum,
        sent,
        got,
        conv_sent,
        conv_got,
        weights,
        weight_t,
        mixed,
        total,
        load_sem,
        table_sem,
        send_sem,
        recv_sem,
        conv_send_sem,
        conv_recv_sem,
        weight_send_sem,
        weight_recv_sem,
        mixed_send_sem,
        mixed_recv_sem,
        partner_send_sem,
        partner_recv_sem,
    ) = rest
    length, channels = query_in.shape
    per_part = length // LANES
    chunk_channels = channels // CHUNKS
    slab = chunk_channels // parts * per_part
    outs = weights.shape[2]
    me = lax.axis_index("seq")
    lane = lax.axis_index("ch")
    core = lax.rem(lane, 2)
    own_y = lane // 2
    partner = lane + 1 - 2 * core
    own_half = pl.multiple_of(core * (outs // 2), outs // 2)
    partner_half = pl.multiple_of((1 - core) * (outs // 2), outs // 2)

    loads = [
        pltpu.make_async_copy(source, target, load_sem.at[number])
        for number, (source, target) in enumerate(
            [
                (filter_hbm, filter_in),
                (skip_hbm, skip_in),
                (key_hbm, key_in),
                (value_hbm, value_in),
                (query_hbm, query_in),
            ]
        )
    ]
    for load in loads[:4]:
        load.start()

    barrier = pltpu.get_barrier_semaphore()

    @pl.loop(1, parts)
    def _(step):
        pl.semaphore_signal(
            barrier, inc=1, device_id={"seq": lax.rem(me + step, parts)}, device_id_type=MESH
        )

    @pl.loop(1, ys)
    def _(step):
        pl.semaphore_signal(
            barrier, inc=1, device_id={"ch": lax.rem(lane + 2 * step, 2 * ys)}, device_id_type=MESH
        )

    pl.semaphore_signal(barrier, inc=1, device_id={"ch": partner}, device_id_type=MESH)

    loads[4].start()
    table_loads = [
        pltpu.make_async_copy(source, target, table_sem.at[number])
        for number, (source, target) in enumerate(zip(table_hbm, table_ref))
    ]
    for load in table_loads:
        load.start()

    def place(source, which, columns):
        for row in range(per_part):
            block = source(pl.ds(row * LANES, LANES), pl.ds(columns, LANES))
            sent[which, pl.ds(columns * per_part + row, LANES, stride=per_part), :] = block.T

    for load in loads[:4]:
        load.wait()
    tap = jnp.where(me == 0, 1.0, 0.0).astype(jnp.float32)
    filter_in[0:1, :] = filter_in[0:1, :] + tap * skip_in[...]

    def send_chunk(chunk):
        def slab_of(peer):
            start = pl.multiple_of(chunk * parts * slab + peer * slab, slab)
            return sent.at[:, pl.ds(start, slab), :]

        @pl.loop(1, parts)
        def _(step):
            peer = lax.rem(me + step, parts)
            pltpu.make_async_remote_copy(
                src_ref=slab_of(peer),
                dst_ref=got.at[:, chunk, me],
                send_sem=send_sem.at[0, chunk],
                recv_sem=recv_sem.at[0, chunk],
                device_id={"seq": peer},
                device_id_type=MESH,
            ).start()

        pltpu.make_async_copy(slab_of(me), got.at[:, chunk, me], recv_sem.at[0, chunk]).start()

    def gated(rows, columns):
        return key_in[rows, columns] * value_in[rows, columns]

    def plain(rows, columns):
        return filter_in[rows, columns]

    def weight_copy(step):
        peer_y = lax.rem(own_y + step, ys)
        start = pl.multiple_of(peer_y * outs, outs)
        return pltpu.make_async_remote_copy(
            src_ref=weight_hbm.at[:, pl.ds(start, outs)],
            dst_ref=weights.at[own_y],
            send_sem=weight_send_sem.at[step - 1],
            recv_sem=weight_recv_sem.at[step - 1],
            device_id={"ch": lax.rem(lane + 2 * step, 2 * ys)},
            device_id_type=MESH,
        )

    own_weight = pltpu.make_async_copy(
        weight_hbm.at[:, pl.ds(pl.multiple_of(own_y * outs, outs), outs)],
        weights.at[own_y],
        weight_recv_sem.at[ys - 1],
    )
    sent_chunks = 0
    for columns in range(0, channels, LANES):
        place(plain, 1, columns)
        place(gated, 0, columns)
        if columns == 0:
            pl.semaphore_wait(barrier, parts - 1 + ys - 1 + 1)
            for step in range(1, ys):
                weight_copy(step).start()
            own_weight.start()
        while (sent_chunks + 1) * chunk_channels <= columns + LANES:
            if sent_chunks < CHUNKS - HELD:
                send_chunk(sent_chunks)
            sent_chunks += 1

    loads[4].wait()
    for columns in range(0, channels, LANES):
        for row in range(per_part):
            query_t[pl.ds(columns, LANES), pl.ds(row * LANES, LANES)] = query_in[
                pl.ds(row * LANES, LANES), pl.ds(columns, LANES)
            ].T
    for load in table_loads:
        load.wait()

    first, last, ahead, behind = (
        (table_ref[2 * n][...], table_ref[2 * n + 1][...]) for n in range(4)
    )
    turn_cos, turn_sin = table_ref[8], table_ref[9]

    def prepare_weights():
        own_weight.wait()
        for step in range(1, ys):
            weight_copy(step).wait_recv()

        @pl.loop(0, ys)
        def _(y):
            for chunk in range(CHUNKS):
                for out in range(0, outs, LANES):
                    block = weights[y, pl.ds(chunk * chunk_channels, chunk_channels), pl.ds(out, LANES)].T
                    high, low = split(block)
                    weight_t[y, chunk, pl.ds(out, LANES), :] = jnp.concatenate([high, low, high], axis=1)

    def convolve_chunk(chunk):
        def arrived(which):
            pltpu.make_async_copy(
                got.at[which, chunk], got.at[which, chunk], recv_sem.at[which, chunk]
            ).wait()

        def transformed(which, rows):
            data = got[which, chunk, :, rows, :].reshape(parts * 8, LANES)
            return spectrum(data, first, ahead, turn_cos[...], turn_sin[...])

        both = got.at[:, chunk]
        pltpu.make_async_copy(both, both, recv_sem.at[0, chunk]).wait()

        @pl.loop(0, slab // 8)
        def _(pair):
            rows = pl.ds(pl.multiple_of(pair * 8, 8), 8)
            filter_spectrum[pair] = transformed(1, rows)


        @pl.loop(0, slab // 8)
        def _(pair):
            rows = pl.ds(pl.multiple_of(pair * 8, 8), 8)
            stage = transformed(0, rows)
            gre, gim = stage[:, :LANES], stage[:, LANES:]
            fre, fim = filter_spectrum[pair, :, :LANES], filter_spectrum[pair, :, LANES:]
            product = jnp.concatenate([gre * fre - gim * fim, gre * fim + gim * fre], axis=1)
            done = inverse(product, behind, last, turn_cos[...], turn_sin[...])
            conv_sent[chunk, :, rows, :] = done.reshape(parts, 8, LANES)

        place_at = pl.ds(pl.multiple_of(me * slab, slab), slab)

        @pl.loop(1, parts)
        def _(step):
            peer = lax.rem(me + step, parts)
            pltpu.make_async_remote_copy(
                src_ref=conv_sent.at[chunk, peer],
                dst_ref=conv_got.at[chunk, place_at, :],
                send_sem=conv_send_sem.at[chunk],
                recv_sem=conv_recv_sem.at[chunk],
                device_id={"seq": peer},
                device_id_type=MESH,
            ).start()

        pltpu.make_async_copy(
            conv_sent.at[chunk, me], conv_got.at[chunk, place_at, :], conv_recv_sem.at[chunk]
        ).start()

        @pl.when(chunk < HELD)
        def _():
            send_chunk(chunk + CHUNKS - HELD)

    total[...] = jnp.zeros_like(total)

    ahead_y, behind_y = lax.rem(own_y + 1, ys), lax.rem(own_y + ys - 1, ys)
    across_y = lax.rem(own_y + 2, ys)
    half_rows = chunk_channels // 2

    def mixed_copy(chunk, owner, half, up, slot):
        return pltpu.make_async_remote_copy(
            src_ref=mixed.at[owner, chunk, pl.ds(half * half_rows, half_rows), :],
            dst_ref=mixed.at[owner, chunk, pl.ds(half * half_rows, half_rows), :],
            send_sem=mixed_send_sem.at[chunk, slot],
            recv_sem=mixed_recv_sem.at[chunk, slot],
            device_id={"ch": lax.rem(lane + (2 if up else 2 * ys - 2), 2 * ys)},
            device_id_type=MESH,
        )

    def own_copies(chunk):
        return [
            mixed_copy(chunk, own_y, 0, True, 0),
            mixed_copy(chunk, own_y, 1, False, 1),
            mixed_copy(chunk, own_y, 1, True, 2),
            mixed_copy(chunk, own_y, 0, False, 3),
        ]

    def relay_copies(chunk):
        return [
            mixed_copy(chunk, behind_y, 0, True, 4),
            mixed_copy(chunk, ahead_y, 1, False, 5),
        ]

    def project(y, chunk):
        high, low = split(mixed[y, chunk])
        data = jnp.concatenate([high, high, low], axis=0)
        total[...] += dot(weight_t[y, chunk], data)

    def relay(chunk):
        mixed_copy(chunk, own_y, 0, True, 0).wait_recv()
        mixed_copy(chunk, behind_y, 0, True, 4).start()
        mixed_copy(chunk, own_y, 1, False, 1).wait_recv()
        mixed_copy(chunk, ahead_y, 1, False, 5).start()

    quarter = outs // 4

    def to_partner(part):
        return pltpu.make_async_remote_copy(
            src_ref=total.at[pl.ds(partner_half + part * quarter, quarter), :],
            dst_ref=partner_got.at[pl.ds(part * quarter, quarter), :],
            send_sem=partner_send_sem.at[part],
            recv_sem=partner_recv_sem.at[part],
            device_id={"ch": partner},
            device_id_type=MESH,
        )

    def finish(chunk, final=False):
        mixed_copy(chunk, own_y, 1, True, 2).wait_recv()
        project(behind_y, chunk)
        mixed_copy(chunk, own_y, 0, False, 3).wait_recv()
        project(ahead_y, chunk)
        for copy in relay_copies(chunk):
            copy.wait_recv()
        if not final:
            project(across_y, chunk)
            return
        high, low = split(mixed[across_y, chunk])
        data = jnp.concatenate([high, high, low], axis=0)
        for part in range(2):
            rows = pl.ds(partner_half + part * quarter, quarter)
            total[rows, :] += dot(weight_t[across_y, chunk, rows, :], data)
            to_partner(part).start()
        rows = pl.ds(own_half, outs // 2)
        out_ref[...] = total[rows, :] + dot(weight_t[across_y, chunk, rows, :], data)

    def gather(chunk):
        pltpu.make_async_copy(
            conv_got.at[chunk], conv_got.at[chunk], conv_recv_sem.at[chunk]
        ).wait()
        for row in range(per_part):
            rows = pl.ds(pl.multiple_of(chunk * chunk_channels, chunk_channels), chunk_channels)
            columns = pl.ds(row * LANES, LANES)
            mixed[own_y, chunk, :, columns] = (
                conv_got[chunk, pl.ds(row, chunk_channels, stride=per_part), :]
                * query_t[rows, columns]
            )
        for copy in own_copies(chunk):
            copy.start()

    @pl.loop(0, CHUNKS + LAG)
    def _(step):
        @pl.when(step < CHUNKS)
        def _():
            convolve_chunk(step)

        @pl.when((step < CHUNKS) & (step > LAG))
        def _():
            relay(step - LAG - 1)

        @pl.when(step >= LAG)
        def _():
            gather(step - LAG)

        @pl.when(step == LAG)
        def _():
            prepare_weights()

        @pl.when((step >= CHUNKS) & (step > LAG))
        def _():
            relay(step - LAG - 1)

        @pl.when(step >= LAG)
        def _():
            project(own_y, step - LAG)

        @pl.when(step > LAG + 1)
        def _():
            finish(step - LAG - 2)

    relay(CHUNKS - 1)
    finish(CHUNKS - 2)
    finish(CHUNKS - 1, final=True)


    @pl.loop(0, CHUNKS)
    def _(chunk):
        rest_of = got.at[:, chunk, pl.ds(0, parts - 1)]
        pltpu.make_async_copy(rest_of, rest_of, send_sem.at[0, chunk]).wait()
        rest_of = conv_sent.at[chunk, pl.ds(0, parts - 1)]
        pltpu.make_async_copy(rest_of, rest_of, conv_send_sem.at[chunk]).wait()
        for copy in own_copies(chunk) + relay_copies(chunk):
            copy.wait_send()

    for step in range(1, ys):
        weight_copy(step).wait_send()
    for part in range(2):
        to_partner(part).wait()


def per_device(query_rows, key_rows, value_rows, filters, skip_gain, out_weight):
    parts = lax.axis_size("seq")
    ys = lax.axis_size("ch") // 2
    length, channels = query_rows.shape
    per_part = length // LANES
    outs = out_weight.shape[1] // ys
    chunk_channels = channels // CHUNKS
    slab = chunk_channels // parts * per_part
    consts = tables(parts, per_part)
    f32 = jnp.float32
    dma = pltpu.SemaphoreType.DMA
    own, other = pl.pallas_call(
        functools.partial(kernel, parts, ys),
        out_shape=[pltpu.VMEM((outs // 2, length), f32)] * 2,
        in_specs=[pl.BlockSpec(memory_space=pl.ANY)] * (6 + len(consts)),
        out_specs=[pl.BlockSpec(memory_space=pltpu.VMEM)] * 2,
        scratch_shapes=[
            *[pltpu.VMEM(table.shape, table.dtype) for table in consts],
            pltpu.VMEM((length, channels), f32),
            pltpu.VMEM((length, channels), f32),
            pltpu.VMEM((length, channels), f32),
            pltpu.VMEM((length, channels), f32),
            pltpu.VMEM((1, channels), f32),
            pltpu.VMEM((channels, length), f32),
            pltpu.VMEM((slab // 8, 2 * parts * per_part, 2 * LANES), f32),
            pltpu.VMEM((2, channels * per_part, LANES), f32),
            pltpu.VMEM((2, CHUNKS, parts, slab, LANES), f32),
            pltpu.VMEM((CHUNKS, parts, slab, LANES), f32),
            pltpu.VMEM((CHUNKS, parts * slab, LANES), f32),
            pltpu.VMEM((ys, channels, outs), f32),
            pltpu.VMEM((ys, CHUNKS, outs, 3 * chunk_channels), jnp.bfloat16),
            pltpu.VMEM((ys, CHUNKS, chunk_channels, length), f32),
            pltpu.VMEM((outs, length), f32),
            dma((5,)),
            dma((len(consts),)),
            dma((2, CHUNKS)),
            dma((2, CHUNKS)),
            dma((CHUNKS,)),
            dma((CHUNKS,)),
            dma((ys - 1,)),
            dma((ys,)),
            dma((CHUNKS, 6)),
            dma((CHUNKS, 6)),
            dma((2,)),
            dma((2,)),
        ],
        compiler_params=pltpu.CompilerParams(collective_id=0, has_side_effects=True),
    )(
        query_rows,
        key_rows,
        value_rows,
        filters,
        skip_gain.reshape(1, channels),
        out_weight,
        *[jnp.asarray(table) for table in consts],
    )
    return own + other


def solution(mesh):
    in_specs = (
        P("seq", "ch"),
        P("seq", "ch"),
        P("seq", "ch"),
        P("seq", "ch"),
        P("ch"),
        P("ch", None),
    )
    out_specs = P("ch", "seq")
    return jax.shard_map(
        per_device, mesh=mesh, in_specs=in_specs, out_specs=out_specs, check_vma=False
    )
```
